512 devices in a mesh: ctx: 64 (over x, z, core), head: 8 (over y).
Axes of the slice: x: 4, y: 8, z: 8, core: 2. Of those that a mesh axis runs over, the one named last changes fastest.
Arguments:
- dec_states: bfloat16 [16384, 4096], P('ctx', 'head'), may hold values from -512 to 512
- norm_gain: float32 [4096], replicated, may hold values from 0.1 to 1.9
- w_query: bfloat16 [4096, 4096], P('ctx', 'head'), may hold values from -0.09375 to 0.09375
- enc_keys: bfloat16 [131072, 4096], P('ctx', 'head'), may hold values from -128 to 128
- enc_values: bfloat16 [131072, 4096], P('ctx', 'head'), may hold values from -24 to 24
- w_out: bfloat16 [4096, 4096], P('ctx', 'head'), may hold values from -0.09375 to 0.09375
- tgt_lengths: int32 [32], replicated, may hold values from 1 to 512, 8192 in all
- src_lengths: int32 [32], replicated, may hold values from 2049 to 4096, as said below
Outputs:
- attn_output: bfloat16 [16384, 4096], P('ctx', 'head')
The draws below stay inside these ranges and needn't reach their ends.
Inputs may be any that keep to these rules, and one draw needn't show every extreme that they name: `tgt_lengths`: the lengths sum to 8192, and the longest equals 512. `src_lengths`: every example has more than 2048 encoder rows, and some example has all 4096.
All inputs are finite; a program needn't handle non-finite values.
Results may differ from the reference program's by a relative error of at most 0.009.
Values may be sent and summed in bfloat16 or wider, within the bound.
No kernel may reach another device: no remote copies, remote signals or barrier semaphores. Data moves between devices by JAX's collectives and lax.ppermute only.
A program may use at most 64 MiB of HBM per device.

```python
import math
import jax
import jax.numpy as jnp
import numpy as np
from jax import lax

D = 4096
DK = 64
PAD_DEV = 256
ENC_DEV = 2048
HD = 4096
EXAMPLES = 32
MAXLEN = 512
ENC_LEN = 4096
ROWS = 16384
ENC_ROWS = 131072


def draw_dec_states(key, part):
    key_one = jax.random.fold_in(key, 11)
    key_two = jax.random.fold_in(key, 12)
    values = jax.random.normal(key_one, (ROWS, D), jnp.float32)
    column_scale = jnp.exp(jax.random.uniform(key_two, (D,), jnp.float32, math.log(0.3), math.log(3.0)))
    values = values * column_scale[None, :]
    return jnp.clip(values, -512.0, 512.0).astype(jnp.bfloat16)


def draw_enc_keys(key, part):
    key_one = jax.random.fold_in(key, 21)
    base = 0.25 * jax.random.normal(key_one, (ENC_ROWS, HD), jnp.float32)
    return jnp.clip(base, -128.0, 128.0).astype(jnp.bfloat16)


def draw_src_lengths(key, part):
    key_one = jax.random.fold_in(key, 31)
    key_two = jax.random.fold_in(key, 32)
    lengths = jax.random.randint(key_one, (EXAMPLES,), ENC_DEV + 1, ENC_LEN + 1, dtype=jnp.int32)
    chosen = jax.random.randint(key_two, (), 0, EXAMPLES, dtype=jnp.int32)
    return jnp.where(jnp.arange(EXAMPLES, dtype=jnp.int32) == chosen, ENC_LEN, lengths).astype(jnp.int32)


def levels(rng, shape, pieces, low, high):
    factor_of = 1.0
    for axis_at, shards_of in pieces:
        heights = jax.random.uniform(jax.random.fold_in(jax.random.fold_in(rng, 6), axis_at), (shards_of,), jnp.float32, low / len(pieces), high / len(pieces))
        factor_of = factor_of * jnp.repeat(jnp.exp(heights), shape[axis_at] // shards_of).reshape((-1,) + (1,) * (len(shape) - 1 - axis_at))
    return factor_of


def split_up(number_of, total, reach, skew):
    portions = [(1 << 20) // math.isqrt(standing ** skew) + 1 for standing in range(2, number_of + 1)]
    spare, holding = total - reach - (number_of - 1), [1] * (number_of - 1)
    while spare > 0:
        free = [i for i in range(number_of - 1) if holding[i] < reach]
        mass, remaining = sum([portions[i] for i in free]), spare
        for i in free:
            extra = min(reach - holding[i], max(1, remaining * portions[i] // mass), spare)
            holding[i] = holding[i] + extra
            spare = spare - extra
    return np.array([reach] + holding)


def uneven_parts(own_key, number_of, total, limit, slope):
    if number_of == 2:
        one = jax.random.randint(own_key, (), max(1, total - limit), min(limit, total - 1) + 1)
        return jnp.stack([one, total - one])
    sizes = jnp.asarray(split_up(number_of, total, limit, slope), jnp.int32)
    pairs = (number_of - 1) // 2
    giver, taker = sizes[1:1 + 2 * pairs:2], sizes[2:2 + 2 * pairs:2]
    margin = jnp.minimum(giver - 1, limit - taker)
    moved = jax.random.randint(jax.random.fold_in(own_key, 1), (pairs,), 0, 1 << 20) % (margin + 1)
    sizes = sizes.at[1:1 + 2 * pairs:2].set(giver - moved).at[2:2 + 2 * pairs:2].set(taker + moved)
    return sizes[jax.random.permutation(jax.random.fold_in(own_key, 2), number_of)]


def normal_values(key, dims, scale, limit, split=(), held_as=jnp.bfloat16):
    level = levels(key, dims, split, -0.22, 0.18) if split else 1.0
    entries = jax.random.normal(key, dims, jnp.float32) * scale * level
    return jnp.minimum(jnp.maximum(entries, -limit), limit).astype(held_as)


def setup_inputs(seed: int = 0) -> dict:
    seeds = jax.random.split(jax.random.key(seed), 9)
    dec_states = draw_dec_states(jax.random.fold_in(seeds[8], 71), 0)
    norm_gain = jnp.clip(1.0 + 0.18 * jax.random.normal(seeds[1], (D,), jnp.float32), 0.1, 1.9)
    w_query = normal_values(seeds[2], (D, HD), D ** -0.5, 0.09375, ((0, 64), (1, 8)))
    enc_keys = draw_enc_keys(jax.random.fold_in(seeds[8], 71), 0)
    enc_values = normal_values(seeds[4], (ENC_ROWS, HD), 4.0, 24.0, ((0, 64), (1, 8)))
    w_out = normal_values(seeds[5], (HD, D), HD ** -0.5, 0.09375, ((0, 64), (1, 8)))
    tgt_lengths = uneven_parts(seeds[6], EXAMPLES, EXAMPLES * PAD_DEV, MAXLEN, 2).astype(jnp.int32)
    src_lengths = draw_src_lengths(jax.random.fold_in(seeds[8], 71), 0)
    return dict(dec_states=dec_states, norm_gain=norm_gain, w_query=w_query, enc_keys=enc_keys, enc_values=enc_values, w_out=w_out, tgt_lengths=tgt_lengths, src_lengths=src_lengths)


def attend(queries, keys, values, key_valid):
    row_count = queries.shape[0]
    head_count = queries.shape[1] // DK
    query_heads = jnp.moveaxis(queries.reshape(row_count, head_count, DK), 1, 0)
    key_heads = jnp.moveaxis(keys.reshape(-1, head_count, DK), 1, 0)
    value_heads = jnp.moveaxis(values.reshape(-1, head_count, DK), 1, 0)

    def one_head(head_items):
        query_head, key_head, value_head = head_items
        scores = jnp.dot(query_head, key_head.T, preferred_element_type=jnp.float32)
        scores = jnp.where(key_valid[None, :], scores, -jnp.inf)
        top_score = lax.optimization_barrier(jnp.max(scores, axis=1))
        weights = jnp.exp(scores - top_score[:, None]).astype(jnp.bfloat16)
        totals = lax.optimization_barrier(jnp.sum(weights.astype(jnp.float32), axis=1))
        weighted = jnp.dot(weights, value_head, preferred_element_type=jnp.float32)
        return (top_score, totals, weighted)
    top_score, totals, weighted = lax.map(one_head, (query_heads, key_heads, value_heads))
    return (top_score.T, totals.T, jnp.moveaxis(weighted, 0, 1).reshape(row_count, head_count * DK))

def combine_halves(first, second):
    top_one, totals_one, weighted_one = first
    top_two, totals_two, weighted_two = second
    row_count = weighted_one.shape[0]
    head_count = top_one.shape[1]
    largest = jnp.maximum(top_one, top_two)
    scale_one = jnp.exp(top_one - largest)
    scale_two = jnp.exp(top_two - largest)
    numer = weighted_one.reshape(row_count, head_count, DK) * scale_one[:, :, None] + weighted_two.reshape(row_count, head_count, DK) * scale_two[:, :, None]
    denom = totals_one * scale_one + totals_two * scale_two
    return (numer / denom[:, :, None]).reshape(row_count, head_count * DK)

def reference(dec_states, norm_gain, w_query, enc_keys, enc_values, w_out, tgt_lengths, src_lengths):
    states = dec_states.astype(jnp.float32)
    normed = (states * lax.rsqrt(lax.optimization_barrier(jnp.mean(states * states, axis=-1, keepdims=True)) + 1e-06) * norm_gain).astype(jnp.bfloat16)
    queries = jnp.dot(normed, w_query, preferred_element_type=jnp.float32).astype(jnp.bfloat16)
    query_blocks = queries.reshape(EXAMPLES, MAXLEN, HD)
    key_blocks = enc_keys.reshape(EXAMPLES, ENC_LEN, HD)
    value_blocks = enc_values.reshape(EXAMPLES, ENC_LEN, HD)

    def one_example(example_items):
        query_ex, key_ex, value_ex, tgt_len, src_len = example_items
        positions = jnp.arange(ENC_DEV, dtype=jnp.int32)
        first = attend(query_ex, key_ex[:ENC_DEV], value_ex[:ENC_DEV], positions < src_len)
        second = attend(query_ex, key_ex[ENC_DEV:], value_ex[ENC_DEV:], positions + ENC_DEV < src_len)
        attended = combine_halves(first, second)
        live_rows = jnp.arange(MAXLEN, dtype=jnp.int32) < tgt_len
        return jnp.where(live_rows[:, None], attended, 0.0).astype(jnp.bfloat16)
    attended = lax.map(one_example, (query_blocks, key_blocks, value_blocks, tgt_lengths, src_lengths))
    attended = attended.reshape(ROWS, HD)
    return jnp.dot(attended, w_out, preferred_element_type=jnp.float32).astype(jnp.bfloat16)
```

```python
import functools

import jax
import jax.numpy as jnp
from jax import lax
from jax.experimental import pallas as pl
from jax.experimental.pallas import tpu as pltpu
from jax.sharding import PartitionSpec as P

DK = 64
NX, NZ = 4, 8


def place(x, z, core):
    return ((x % NX) * NZ + z % NZ) * 2 + core


def along_x(shift):
    return [
        (place(x, z, core), place(x + shift, z, core))
        for x in range(NX)
        for z in range(NZ)
        for core in range(2)
    ]


PARTNERS = [(i, i ^ 1) for i in range(2 * NX * NZ)]
Z_GROUPS = [[place(x, z, core) for z in range(NZ)] for x in range(NX) for core in range(2)]
X_GROUPS = [[place(x, z, core) for x in range(NX)] for z in range(NZ) for core in range(2)]


def fill_weights(idx_ref, own_ref, far_ref, w, sems):
    copies = []
    for i in range(NX):
        copies.append(
            pltpu.make_async_copy(own_ref.at[i], w.at[idx_ref[i], :, idx_ref[NX]], sems.at[i])
        )
        copies.append(
            pltpu.make_async_copy(
                far_ref.at[i], w.at[idx_ref[i], :, 1 - idx_ref[NX]], sems.at[NX + i]
            )
        )
    return copies


def project_kernel(normalize, idx_ref, x_ref, gain_ref, own_ref, far_ref, o_ref, xs, w, sems):
    blocks, rows, width = xs.shape
    copies = fill_weights(idx_ref, own_ref, far_ref, w, sems)
    load = pltpu.make_async_copy(x_ref, xs, sems.at[2 * NX])
    load.start()
    for copy in copies:
        copy.start()
    load.wait()
    if normalize:
        square = jnp.zeros((rows, width), jnp.float32)
        for b in range(blocks):
            part = xs[b].astype(jnp.float32)
            square = square + part * part
        mean = jnp.sum(square, axis=1, keepdims=True) / (blocks * width)
        scale = lax.rsqrt(mean + 1e-06)
        for b in range(blocks):
            part = xs[b].astype(jnp.float32)
            xs[b] = (part * scale * gain_ref[b]).astype(jnp.bfloat16)
    for copy in copies:
        copy.wait()
    acc = jnp.zeros(o_ref.shape, jnp.float32)
    for b in range(blocks):
        depth = NZ * NX // blocks
        at = b * depth
        part = w[at // NZ, at % NZ : at % NZ + depth].reshape(width, o_ref.shape[1])
        acc = acc + jnp.dot(xs[b], part, preferred_element_type=jnp.float32)
    o_ref[...] = acc.astype(jnp.bfloat16)


def project(normalize, idx, x, gain, own, far):
    blocks, rows, width = x.shape
    piece = own.shape[2]
    out = own.shape[3]
    anywhere = pl.BlockSpec(memory_space=pl.ANY)
    return pl.pallas_call(
        functools.partial(project_kernel, normalize),
        out_shape=jax.ShapeDtypeStruct((rows, out), jnp.bfloat16),
        grid_spec=pltpu.PrefetchScalarGridSpec(
            num_scalar_prefetch=1,
            grid=(1,),
            in_specs=[
                anywhere,
                pl.BlockSpec((blocks, 1, width), lambda i, s: (0, 0, 0)),
                anywhere,
                anywhere,
            ],
            out_specs=pl.BlockSpec((rows, out), lambda i, s: (0, 0)),
            scratch_shapes=[
                pltpu.VMEM((blocks, rows, width), jnp.bfloat16),
                pltpu.VMEM((NX, NZ, 2, piece, out), jnp.bfloat16),
                pltpu.SemaphoreType.DMA((2 * NX + 1,)),
            ],
        ),
        compiler_params=pltpu.CompilerParams(vmem_limit_bytes=32 << 20),
        cost_estimate=pl.CostEstimate(
            flops=2 * rows * blocks * width * out,
            bytes_accessed=2 * blocks * width * (rows + out),
            transcendentals=0,
        ),
        name="project",
    )(idx, x, gain, own, far)


def attend_kernel(step, s_ref, q_ref, ko_ref, vo_ref, kf_ref, vf_ref, o_ref, keys, val_a, val_b):
    half = ko_ref.shape[0]
    rows = q_ref.shape[0]
    tile = 256
    first = lax.broadcasted_iota(jnp.int32, (1, 2 * DK), 1) < DK
    sides = ((0, ko_ref, vo_ref, s_ref[0]), (half, kf_ref, vf_ref, s_ref[1]))
    for base, k_ref, v_ref, count in sides:
        for c in range(0, half, tile):
            valid = lax.broadcasted_iota(jnp.int32, (tile, 1), 0) + c < count
            there = slice(base + c, base + c + tile)
            keys[there, :] = jnp.where(valid, k_ref[c : c + tile, :], k_ref[0:1, :])
            v = v_ref[c : c + tile, :]
            one, zero = jnp.ones_like(v), jnp.zeros_like(v)
            val_a[there, :] = jnp.where(valid, jnp.where(first, v, one), zero)
            val_b[there, :] = jnp.where(valid, jnp.where(first, one, v), zero)
    q = q_ref[...]
    parts = []
    for mine, values in ((first, val_a), (~first, val_b)):
        q_head = jnp.where(mine, q, jnp.zeros_like(q))
        top = acc = None
        for c in range(0, 2 * half, step):
            scores = lax.dot_general(
                q_head,
                keys[c : c + step, :],
                (((1,), (1,)), ((), ())),
                preferred_element_type=jnp.float32,
            )
            new_top = jnp.max(scores, axis=1, keepdims=True)
            if top is not None:
                new_top = jnp.maximum(top, new_top)
            weights = jnp.exp(scores - new_top).astype(jnp.bfloat16)
            part = jnp.dot(weights, values[c : c + step, :], preferred_element_type=jnp.float32)
            acc = part if top is None else acc * jnp.exp(top - new_top) + part
            top = new_top
        parts.append(acc / pltpu.roll(acc, DK, 1))
    live = lax.broadcasted_iota(jnp.int32, (rows, 1), 0) < s_ref[2]
    o_ref[...] = jnp.where(live, jnp.where(first, parts[0], parts[1]), 0.0).astype(jnp.bfloat16)


def attend(counts, q, own_k, own_v, far_k, far_v):
    rows, width = q.shape
    half = own_k.shape[0]
    pair = 2 * DK
    kv = pl.BlockSpec((half, pair), lambda h, s: (0, h))
    qs = pl.BlockSpec((rows, pair), lambda h, s: (0, h))
    return pl.pallas_call(
        functools.partial(attend_kernel, half),
        out_shape=jax.ShapeDtypeStruct((rows, width), jnp.bfloat16),
        grid_spec=pltpu.PrefetchScalarGridSpec(
            num_scalar_prefetch=1,
            grid=(width // pair,),
            in_specs=[qs, kv, kv, kv, kv],
            out_specs=qs,
            scratch_shapes=[pltpu.VMEM((2 * half, pair), jnp.bfloat16)] * 3,
        ),
        compiler_params=pltpu.CompilerParams(vmem_limit_bytes=40 << 20),
        cost_estimate=pl.CostEstimate(
            flops=16 * rows * width * half,
            bytes_accessed=8 * half * width,
            transcendentals=2 * rows * width // DK * half,
        ),
        name="attend",
    )(counts, q, own_k, own_v, far_k, far_v)


def local(dec_states, norm_gain, w_query, enc_keys, enc_values, w_out, tgt_lengths, src_lengths):
    heads = lax.axis_size("head")
    position = lax.axis_index("ctx")
    core = position % 2
    x = position // (2 * NZ)
    example = position // 2
    rows, width = dec_states.shape
    piece = w_query.shape[0]
    enc_count = enc_keys.shape[0]
    slot_ids = jnp.arange(tgt_lengths.shape[0], dtype=jnp.int32)
    tgt_len = jnp.sum(jnp.where(slot_ids == example, tgt_lengths, 0))
    src_len = jnp.sum(jnp.where(slot_ids == example, src_lengths, 0))
    counts = jnp.stack(
        [src_len - core * enc_count, src_len - (1 - core) * enc_count, tgt_len - core * rows]
    ).astype(jnp.int32)

    states = lax.all_gather(dec_states, "head")

    pieces = jnp.broadcast_to(
        jnp.concatenate([w_query, w_out], axis=1)[None], (NZ, piece, 2 * width)
    )
    pieces = lax.all_to_all(pieces, "ctx", 0, 0, axis_index_groups=Z_GROUPS)
    wq_own = pieces[:, :, :width].reshape(NZ * piece, width)
    wo_own = pieces[:, :, width:].reshape(NZ * piece, width)

    far_keys = lax.ppermute(enc_keys, "ctx", PARTNERS)
    far_values = lax.ppermute(enc_values, "ctx", PARTNERS)

    mid = NZ * piece // 2
    ahead = lax.ppermute(wq_own, "ctx", along_x(1))
    behind = lax.ppermute(wq_own, "ctx", along_x(-1))
    last_top = lax.ppermute(ahead[:mid], "ctx", along_x(1))
    last_low = lax.ppermute(behind[mid:], "ctx", along_x(-1))
    wq_core = jnp.concatenate([wq_own, ahead, behind, last_top, last_low], axis=0)
    wq_far = lax.ppermute(wq_core, "ctx", PARTNERS)

    wo_core = lax.all_gather(wo_own, "ctx", axis_index_groups=X_GROUPS)
    wo_core = wo_core.reshape(NX * NZ * piece, width)
    wo_far = lax.ppermute(wo_core, "ctx", PARTNERS)

    blocks = (NX, NZ, piece, width)
    ring = jnp.stack([x, (x - 1) % NX, (x + 1) % NX, (x + 2) % NX, core]).astype(jnp.int32)
    order = jnp.stack([0 * x, 0 * x + 1, 0 * x + 2, 0 * x + 3, core]).astype(jnp.int32)
    gain = norm_gain.reshape(heads, 1, width)
    queries = project(True, ring, states, gain, wq_core.reshape(blocks), wq_far.reshape(blocks))
    attended = attend(counts, queries, enc_keys, enc_values, far_keys, far_values)
    everything = lax.all_gather(attended, "head")
    return project(False, order, everything, gain, wo_core.reshape(blocks), wo_far.reshape(blocks))


def solution(mesh):
    placed = (
        P("ctx", "head"),
        P(),
        P("ctx", "head"),
        P("ctx", "head"),
        P("ctx", "head"),
        P("ctx", "head"),
        P(),
        P(),
    )
    return jax.shard_map(
        local, mesh=mesh, in_specs=placed, out_specs=P("ctx", "head"), check_vma=False
    )
```

```python
import functools

import jax
import jax.numpy as jnp
from jax import lax
from jax.experimental import pallas as pl
from jax.experimental.pallas import tpu as pltpu
from jax.sharding import PartitionSpec as P

DK = 64
NX, NZ = 4, 8
CUTS = (3, 1)


def place(x, z, core):
    return ((x % NX) * NZ + z % NZ) * 2 + core


PARTNERS = [(i, i ^ 1) for i in range(2 * NX * NZ)]
Z_GROUPS = [[place(x, z, core) for z in range(NZ)] for x in range(NX) for core in range(2)]
X_GROUPS = [[place(x, z, core) for x in range(NX)] for z in range(NZ) for core in range(2)]


def project_kernel(normalize, n_in, core_ref, *refs):
    x_refs, (gain_ref, own_ref, far_ref, o_ref, xs, w, sems) = refs[:n_in], refs[n_in:]
    blocks, rows, width = xs.shape
    core = core_ref[0]
    loads, at = [], 0
    for i, x_ref in enumerate(x_refs):
        there = slice(at, at + x_ref.shape[2])
        loads.append(pltpu.make_async_copy(x_ref, xs.at[:, :, there], sems.at[2 * NX + i]))
        at += x_ref.shape[2]
    own = [pltpu.make_async_copy(own_ref.at[i], w.at[i, :, core], sems.at[i]) for i in range(NX)]
    far = [
        pltpu.make_async_copy(far_ref.at[i], w.at[i, :, 1 - core], sems.at[NX + i])
        for i in range(NX)
    ]
    for copy in loads:
        copy.start()
    for i in range(NX):
        own[i].start()
        far[i].start()
    for copy in loads:
        copy.wait()
    if normalize:
        square = jnp.zeros((rows, width), jnp.float32)
        for b in range(blocks):
            part = xs[b].astype(jnp.float32)
            square = square + part * part
        mean = jnp.sum(square, axis=1, keepdims=True) / (blocks * width)
        scale = lax.rsqrt(mean + 1e-06)
        for b in range(blocks):
            part = xs[b].astype(jnp.float32)
            xs[b] = (part * scale * gain_ref[b]).astype(jnp.bfloat16)
    each = blocks // NX
    depth = NZ // each
    acc = jnp.zeros(o_ref.shape, jnp.float32)
    for i in range(NX):
        own[i].wait()
        far[i].wait()
        for j in range(each):
            part = w[i, j * depth : (j + 1) * depth].reshape(width, o_ref.shape[1])
            acc = acc + jnp.dot(xs[i * each + j], part, preferred_element_type=jnp.float32)
    o_ref[...] = acc.astype(jnp.bfloat16)


def project(normalize, core, xs, gain, own, far):
    blocks, rows = xs[0].shape[:2]
    width = sum(x.shape[2] for x in xs)
    piece, out = own.shape[-2:]
    anywhere = pl.BlockSpec(memory_space=pl.ANY)
    return pl.pallas_call(
        functools.partial(project_kernel, normalize, len(xs)),
        out_shape=jax.ShapeDtypeStruct((rows, out), jnp.bfloat16),
        grid_spec=pltpu.PrefetchScalarGridSpec(
            num_scalar_prefetch=1,
            grid=(1,),
            in_specs=[anywhere] * len(xs)
            + [pl.BlockSpec((blocks, 1, width), lambda i, s: (0, 0, 0)), anywhere, anywhere],
            out_specs=pl.BlockSpec((rows, out), lambda i, s: (0, 0)),
            scratch_shapes=[
                pltpu.VMEM((blocks, rows, width), jnp.bfloat16),
                pltpu.VMEM((NX, NZ, 2, piece, out), jnp.bfloat16),
                pltpu.SemaphoreType.DMA((2 * NX + len(xs),)),
            ],
        ),
        compiler_params=pltpu.CompilerParams(vmem_limit_bytes=60 << 20),
        cost_estimate=pl.CostEstimate(
            flops=2 * rows * blocks * width * out,
            bytes_accessed=2 * blocks * width * (rows + out),
            transcendentals=0,
        ),
        name="project",
    )(core, *xs, gain, own, far)


def attend_kernel(step, start, s_ref, q_ref, ko_ref, vo_ref, kf_ref, vf_ref, o_ref, keys, vals, sems):
    half = ko_ref.shape[0]
    rows = q_ref.shape[0]
    pair, tile = 2 * DK, 256
    turn, turns = pl.program_id(0), pl.num_programs(0)
    slot = lax.rem(turn, 2)

    def copies(h, into):
        lanes = pl.ds(pl.multiple_of((start + h) * pair, pair), pair)
        return [
            pltpu.make_async_copy(ko_ref.at[:, lanes], keys.at[into, :half], sems.at[into, 0]),
            pltpu.make_async_copy(kf_ref.at[:, lanes], keys.at[into, half:], sems.at[into, 1]),
            pltpu.make_async_copy(vo_ref.at[:, lanes], vals.at[into, :half, :pair], sems.at[into, 2]),
            pltpu.make_async_copy(vf_ref.at[:, lanes], vals.at[into, half:, :pair], sems.at[into, 3]),
        ]

    @pl.when(turn == 0)
    def _():
        for copy in copies(turn, slot):
            copy.start()
        for base, count in ((0, s_ref[0]), (half, s_ref[1])):
            for c in range(0, half, tile):
                valid = lax.broadcasted_iota(jnp.int32, (tile, pair), 0) + c < count
                ones = jnp.where(valid, 1.0, 0.0).astype(jnp.bfloat16)
                for into in range(2):
                    vals[into, base + c : base + c + tile, pair:] = ones

    @pl.when(turn + 1 < turns)
    def _():
        for copy in copies(turn + 1, 1 - slot):
            copy.start()

    for copy in copies(turn, slot):
        copy.wait()
    for base, count in ((0, s_ref[0]), (half, s_ref[1])):
        for c in range(0, half, tile):

            @pl.when(c + tile > count)
            def _():
                there = slice(base + c, base + c + tile)
                valid = lax.broadcasted_iota(jnp.int32, (tile, 1), 0) + c < count
                keys[slot, there] = jnp.where(valid, keys[slot, there], keys[slot, base : base + 1])
                v = vals[slot, there, :pair]
                vals[slot, there, :pair] = jnp.where(valid, v, jnp.zeros_like(v))
    first = lax.broadcasted_iota(jnp.int32, (1, pair), 1) < DK
    q = q_ref[...]
    zero = jnp.zeros_like(q)
    both = jnp.concatenate([jnp.where(first, q, zero), jnp.where(first, zero, q)], axis=0)
    top = acc = None
    for c in range(0, 2 * half, step):
        scores = lax.dot_general(both, keys[slot, c : c + step], (((1,), (1,)), ((), ())), preferred_element_type=jnp.float32)
        new_top = jnp.max(scores, axis=1, keepdims=True)
        if top is not None:
            new_top = jnp.maximum(top, new_top)
        weights = jnp.exp(scores - new_top).astype(jnp.bfloat16)
        part = jnp.dot(weights, vals[slot, c : c + step], preferred_element_type=jnp.float32)
        acc = part if top is None else acc * jnp.exp(top - new_top) + part
        top = new_top
    out = acc[:, :pair] / acc[:, pair:]
    live = lax.broadcasted_iota(jnp.int32, (rows, 1), 0) < s_ref[2]
    o_ref[...] = jnp.where(live, jnp.where(first, out[:rows], out[rows:]), 0.0).astype(jnp.bfloat16)


def attend(counts, q, own_k, own_v, far_k, far_v, start, pairs):
    rows = q.shape[0]
    width = pairs * 2 * DK
    half = own_k.shape[0]
    pair = 2 * DK
    hbm = pl.BlockSpec(memory_space=pl.ANY)
    qs = pl.BlockSpec((rows, pair), lambda h, s: (0, start + h))
    os = pl.BlockSpec((rows, pair), lambda h, s: (0, h))
    return pl.pallas_call(
        functools.partial(attend_kernel, 512, start),
        out_shape=jax.ShapeDtypeStruct((rows, width), jnp.bfloat16),
        grid_spec=pltpu.PrefetchScalarGridSpec(
            num_scalar_prefetch=1,
            grid=(pairs,),
            in_specs=[qs, hbm, hbm, hbm, hbm],
            out_specs=os,
            scratch_shapes=[
                pltpu.VMEM((2, 2 * half, pair), jnp.bfloat16),
                pltpu.VMEM((2, 2 * half, 2 * pair), jnp.bfloat16),
                pltpu.SemaphoreType.DMA((2, 4)),
            ],
        ),
        compiler_params=pltpu.CompilerParams(vmem_limit_bytes=60 << 20),
        cost_estimate=pl.CostEstimate(
            flops=16 * rows * width * half,
            bytes_accessed=8 * half * width,
            transcendentals=2 * rows * width // DK * half,
        ),
        name="attend",
    )(counts, q, own_k, own_v, far_k, far_v)


def local(dec_states, norm_gain, w_query, enc_keys, enc_values, w_out, tgt_lengths, src_lengths):
    heads = lax.axis_size("head")
    position = lax.axis_index("ctx")
    core = position % 2
    example = position // 2
    rows, width = dec_states.shape
    piece = w_query.shape[0]
    enc_count = enc_keys.shape[0]
    slot_ids = jnp.arange(tgt_lengths.shape[0], dtype=jnp.int32)
    tgt_len = jnp.sum(jnp.where(slot_ids == example, tgt_lengths, 0))
    src_len = jnp.sum(jnp.where(slot_ids == example, src_lengths, 0))
    counts = jnp.stack(
        [src_len - core * enc_count, src_len - (1 - core) * enc_count, tgt_len - core * rows]
    ).astype(jnp.int32)
    side = core.reshape(1).astype(jnp.int32)

    states = lax.all_gather(dec_states, "head")

    pieces = jnp.broadcast_to(
        jnp.concatenate([w_query, w_out], axis=1)[None], (NZ, piece, 2 * width)
    )
    pieces = lax.all_to_all(pieces, "ctx", 0, 0, axis_index_groups=Z_GROUPS)
    wq = pieces[:, :, :width]
    wo = pieces[:, :, width:]
    wo_own = lax.all_gather(wo, "ctx", axis_index_groups=X_GROUPS)

    wq = jnp.broadcast_to(wq[None], (NX, NZ, piece, width))
    wq_own = lax.all_to_all(wq, "ctx", 0, 0, axis_index_groups=X_GROUPS)
    wq_own, states = lax.optimization_barrier((wq_own, states))
    wq_far = lax.ppermute(wq_own, "ctx", PARTNERS)
    wq_own, keys, values = lax.optimization_barrier((wq_own, enc_keys, enc_values))
    far_keys = lax.ppermute(keys, "ctx", PARTNERS)
    far_values = lax.ppermute(values, "ctx", PARTNERS)
    wo_far = lax.ppermute(wo_own, "ctx", PARTNERS)

    gain = norm_gain.reshape(heads, 1, width)
    queries = project(True, side, [states], gain, wq_own, wq_far)
    gathered, start = [], 0
    for pairs in CUTS:
        attended = attend(
            counts, queries, enc_keys, enc_values, far_keys, far_values, start, pairs
        )
        gathered.append(lax.all_gather(attended, "head"))
        start += pairs
    return project(False, side, gathered, gain, wo_own, wo_far)


def solution(mesh):
    placed = (
        P("ctx", "head"),
        P(),
        P("ctx", "head"),
        P("ctx", "head"),
        P("ctx", "head"),
        P("ctx", "head"),
        P(),
        P(),
    )
    return jax.shard_map(
        local, mesh=mesh, in_specs=placed, out_specs=P("ctx", "head"), check_vma=False
    )
```

```python
import functools

import jax
import jax.numpy as jnp
from jax import lax
from jax.experimental import pallas as pl
from jax.experimental.pallas import tpu as pltpu
from jax.sharding import PartitionSpec as P

DK = 64
NX, NZ = 4, 8
CUTS = (3, 1)


def place(x, z, core):
    return ((x % NX) * NZ + z % NZ) * 2 + core


PARTNERS = [(i, i ^ 1) for i in range(2 * NX * NZ)]
Z_GROUPS = [[place(x, z, core) for z in range(NZ)] for x in range(NX) for core in range(2)]
X_GROUPS = [[place(x, z, core) for x in range(NX)] for z in range(NZ) for core in range(2)]


def normalize_kernel(x_ref, gain_ref, o_ref):
    blocks, rows, width = x_ref.shape
    square = jnp.zeros((rows, width), jnp.float32)
    for b in range(blocks):
        part = x_ref[b].astype(jnp.float32)
        square = square + part * part
    mean = jnp.sum(square, axis=1, keepdims=True) / (blocks * width)
    scale = lax.rsqrt(mean + 1e-06)
    first = lax.broadcasted_iota(jnp.int32, (1, 2 * DK), 1) < DK
    for b in range(blocks):
        part = x_ref[b].astype(jnp.float32) * scale * gain_ref[b]
        for j in range(width // (4 * DK)):
            one = part[:, 4 * DK * j : 4 * DK * j + 2 * DK]
            two = part[:, 4 * DK * j + 2 * DK : 4 * DK * (j + 1)]
            lanes = slice(2 * DK * j, 2 * DK * (j + 1))
            even = jnp.where(first, one, pltpu.roll(two, DK, 1))
            odd = jnp.where(first, pltpu.roll(one, DK, 1), two)
            o_ref[0, b, :, lanes] = even.astype(jnp.bfloat16)
            o_ref[1, b, :, lanes] = odd.astype(jnp.bfloat16)


def normalize(x, gain):
    blocks, rows, width = x.shape
    tile = 64
    return pl.pallas_call(
        normalize_kernel,
        out_shape=jax.ShapeDtypeStruct((2, blocks, rows, width // 2), jnp.bfloat16),
        grid=(rows // tile,),
        in_specs=[
            pl.BlockSpec((blocks, tile, width), lambda i: (0, i, 0)),
            pl.BlockSpec((blocks, 1, width), lambda i: (0, 0, 0)),
        ],
        out_specs=pl.BlockSpec((2, blocks, tile, width // 2), lambda i: (0, 0, i, 0)),
        compiler_params=pltpu.CompilerParams(vmem_limit_bytes=58 << 20),
        cost_estimate=pl.CostEstimate(
            flops=8 * rows * blocks * width,
            bytes_accessed=4 * blocks * width * rows,
            transcendentals=rows,
        ),
        name="normalize",
    )(x, gain)


def query_kernel(side_ref, x_ref, w_ref, *refs):
    sum_ref = refs[0] if len(refs) == 5 else None
    o_ref, xs, w, sems = refs[-4:]
    blocks = xs.shape[0]
    each = blocks // NX
    x_copies, w_copies = [], []
    for i in range(NX):
        there = slice(i * each, (i + 1) * each)
        x_copies.append(
            pltpu.make_async_copy(x_ref.at[side_ref[0], there], xs.at[there], sems.at[0, i])
        )
        w_copies.append(pltpu.make_async_copy(w_ref.at[i], w.at[i], sems.at[1, i]))
    for i in range(NX):
        x_copies[i].start()
        w_copies[i].start()
    depth = NZ // each
    total = jnp.zeros(o_ref.shape, jnp.float32) if sum_ref is None else sum_ref[...]
    for i in range(NX):
        x_copies[i].wait()
        w_copies[i].wait()
        for j in range(each):
            part = w[i, j * depth : (j + 1) * depth].reshape(xs.shape[2], o_ref.shape[1])
            total = total + jnp.dot(xs[i * each + j], part, preferred_element_type=jnp.float32)
    o_ref[...] = total.astype(o_ref.dtype)


def query_part(side, x, weights, partial=None):
    _, blocks, rows, half = x.shape
    piece, out = weights.shape[2:]
    whole = pl.BlockSpec((rows, out), lambda i, s: (0, 0))
    anywhere = pl.BlockSpec(memory_space=pl.ANY)
    more = [] if partial is None else [partial]
    return pl.pallas_call(
        query_kernel,
        out_shape=jax.ShapeDtypeStruct(
            (rows, out), jnp.float32 if partial is None else jnp.bfloat16
        ),
        grid_spec=pltpu.PrefetchScalarGridSpec(
            num_scalar_prefetch=1,
            grid=(1,),
            in_specs=[anywhere, anywhere] + [whole] * len(more),
            out_specs=whole,
            scratch_shapes=[
                pltpu.VMEM((blocks, rows, half), jnp.bfloat16),
                pltpu.VMEM((NX, NZ, piece, out), jnp.bfloat16),
                pltpu.SemaphoreType.DMA((2, NX)),
            ],
        ),
        compiler_params=pltpu.CompilerParams(vmem_limit_bytes=24 << 20),
        cost_estimate=pl.CostEstimate(
            flops=2 * rows * blocks * half * out,
            bytes_accessed=2 * blocks * half * (rows + out),
            transcendentals=0,
        ),
        name="query_part",
    )(side, x, weights, *more)


def output_kernel(n_in, side_ref, *refs):
    x_refs, (own_ref, far_ref, o_ref, xs, w, sems) = refs[:n_in], refs[n_in:]
    blocks, _, width = xs.shape
    core = side_ref[0]
    each = blocks // NX
    depth = NZ // each
    copies = []
    for i in range(NX):
        blocks_of = slice(i * each, (i + 1) * each)
        group, at = [], 0
        for k, x_ref in enumerate(x_refs):
            lanes = slice(at, at + x_ref.shape[2])
            group.append(
                pltpu.make_async_copy(x_ref.at[blocks_of], xs.at[blocks_of, :, lanes], sems.at[i, k])
            )
            at += x_ref.shape[2]
        group.append(pltpu.make_async_copy(own_ref.at[i], w.at[i, :, core], sems.at[i, n_in]))
        group.append(
            pltpu.make_async_copy(far_ref.at[i], w.at[i, :, 1 - core], sems.at[i, n_in + 1])
        )
        copies.append(group)
    for group in copies:
        for copy in group:
            copy.start()
    acc = jnp.zeros(o_ref.shape, jnp.float32)
    for i in range(NX):
        for copy in copies[i]:
            copy.wait()
        for j in range(each):
            part = w[i, j * depth : (j + 1) * depth].reshape(width, o_ref.shape[1])
            acc = acc + jnp.dot(xs[i * each + j], part, preferred_element_type=jnp.float32)
    o_ref[...] = acc.astype(jnp.bfloat16)


def output_product(side, xs, own, far):
    blocks, rows = xs[0].shape[:2]
    width = sum(x.shape[2] for x in xs)
    piece, out = own.shape[2:]
    anywhere = pl.BlockSpec(memory_space=pl.ANY)
    return pl.pallas_call(
        functools.partial(output_kernel, len(xs)),
        out_shape=jax.ShapeDtypeStruct((rows, out), jnp.bfloat16),
        grid_spec=pltpu.PrefetchScalarGridSpec(
            num_scalar_prefetch=1,
            grid=(1,),
            in_specs=[anywhere] * (len(xs) + 2),
            out_specs=pl.BlockSpec((rows, out), lambda i, s: (0, 0)),
            scratch_shapes=[
                pltpu.VMEM((blocks, rows, width), jnp.bfloat16),
                pltpu.VMEM((NX, NZ, 2, piece, out), jnp.bfloat16),
                pltpu.SemaphoreType.DMA((NX, len(xs) + 2)),
            ],
        ),
        compiler_params=pltpu.CompilerParams(vmem_limit_bytes=56 << 20),
        cost_estimate=pl.CostEstimate(
            flops=2 * rows * blocks * width * out,
            bytes_accessed=2 * blocks * width * (rows + out),
            transcendentals=0,
        ),
        name="output_product",
    )(side, *xs, own, far)


def attend_kernel(step, start, s_ref, q_ref, ko_ref, vo_ref, kf_ref, vf_ref, o_ref, keys, vals, sems):
    half = ko_ref.shape[0]
    rows = q_ref.shape[0]
    pair, tile = 2 * DK, 256
    turn, turns = pl.program_id(0), pl.num_programs(0)
    slot = lax.rem(turn, 2)

    def copies(h, into):
        lanes = pl.ds(pl.multiple_of((start + h) * pair, pair), pair)
        return [
            pltpu.make_async_copy(ko_ref.at[:, lanes], keys.at[into, :half], sems.at[into, 0]),
            pltpu.make_async_copy(kf_ref.at[:, lanes], keys.at[into, half:], sems.at[into, 1]),
            pltpu.make_async_copy(vo_ref.at[:, lanes], vals.at[into, :half, :pair], sems.at[into, 2]),
            pltpu.make_async_copy(vf_ref.at[:, lanes], vals.at[into, half:, :pair], sems.at[into, 3]),
        ]

    @pl.when(turn == 0)
    def _():
        for copy in copies(turn, slot):
            copy.start()
        for base, count in ((0, s_ref[0]), (half, s_ref[1])):
            for c in range(0, half, tile):
                valid = lax.broadcasted_iota(jnp.int32, (tile, pair), 0) + c < count
                ones = jnp.where(valid, 1.0, 0.0).astype(jnp.bfloat16)
                for into in range(2):
                    vals[into, base + c : base + c + tile, pair:] = ones

    @pl.when(turn + 1 < turns)
    def _():
        for copy in copies(turn + 1, 1 - slot):
            copy.start()

    def arrive(k, base, count):
        for copy in (copies(turn, slot)[k], copies(turn, slot)[k + 2]):
            copy.wait()
        for c in range(0, half, tile):

            @pl.when(c + tile > count)
            def _():
                there = slice(base + c, base + c + tile)
                valid = lax.broadcasted_iota(jnp.int32, (tile, 1), 0) + c < count
                keys[slot, there] = jnp.where(valid, keys[slot, there], keys[slot, base : base + 1])
                v = vals[slot, there, :pair]
                vals[slot, there, :pair] = jnp.where(valid, v, jnp.zeros_like(v))

    first = lax.broadcasted_iota(jnp.int32, (1, pair), 1) < DK
    q = q_ref[...]
    zero = jnp.zeros_like(q)
    both = jnp.concatenate([jnp.where(first, q, zero), jnp.where(first, zero, q)], axis=0)
    top = acc = None
    for c in range(0, 2 * half, step):
        if c == 0:
            arrive(0, 0, s_ref[0])
        if c == half:
            arrive(1, half, s_ref[1])
        scores = lax.dot_general(both, keys[slot, c : c + step], (((1,), (1,)), ((), ())), preferred_element_type=jnp.float32)
        new_top = jnp.max(scores, axis=1, keepdims=True)
        if top is not None:
            new_top = jnp.maximum(top, new_top)
        weights = jnp.exp(scores - new_top).astype(jnp.bfloat16)
        part = jnp.dot(weights, vals[slot, c : c + step], preferred_element_type=jnp.float32)
        acc = part if top is None else acc * jnp.exp(top - new_top) + part
        top = new_top
    out = acc[:, :pair] / acc[:, pair:]
    live = lax.broadcasted_iota(jnp.int32, (rows, 1), 0) < s_ref[2]
    o_ref[...] = jnp.where(live, jnp.where(first, out[:rows], out[rows:]), 0.0).astype(jnp.bfloat16)


def attend(counts, q, own_k, own_v, far_k, far_v, start, pairs):
    rows = q.shape[0]
    width = pairs * 2 * DK
    half = own_k.shape[0]
    pair = 2 * DK
    hbm = pl.BlockSpec(memory_space=pl.ANY)
    qs = pl.BlockSpec((rows, pair), lambda h, s: (0, start + h))
    os = pl.BlockSpec((rows, pair), lambda h, s: (0, h))
    return pl.pallas_call(
        functools.partial(attend_kernel, 512, start),
        out_shape=jax.ShapeDtypeStruct((rows, width), jnp.bfloat16),
        grid_spec=pltpu.PrefetchScalarGridSpec(
            num_scalar_prefetch=1,
            grid=(pairs,),
            in_specs=[qs, hbm, hbm, hbm, hbm],
            out_specs=os,
            scratch_shapes=[
                pltpu.VMEM((2, 2 * half, pair), jnp.bfloat16),
                pltpu.VMEM((2, 2 * half, 2 * pair), jnp.bfloat16),
                pltpu.SemaphoreType.DMA((2, 4)),
            ],
        ),
        compiler_params=pltpu.CompilerParams(vmem_limit_bytes=58 << 20),
        cost_estimate=pl.CostEstimate(
            flops=16 * rows * width * half,
            bytes_accessed=8 * half * width,
            transcendentals=2 * rows * width // DK * half,
        ),
        name="attend",
    )(counts, q, own_k, own_v, far_k, far_v)


def local(dec_states, norm_gain, w_query, enc_keys, enc_values, w_out, tgt_lengths, src_lengths):
    heads = lax.axis_size("head")
    position = lax.axis_index("ctx")
    core = position % 2
    example = position // 2
    rows, width = dec_states.shape
    piece = w_query.shape[0]
    enc_count = enc_keys.shape[0]
    slot_ids = jnp.arange(tgt_lengths.shape[0], dtype=jnp.int32)
    tgt_len = jnp.sum(jnp.where(slot_ids == example, tgt_lengths, 0))
    src_len = jnp.sum(jnp.where(slot_ids == example, src_lengths, 0))
    counts = jnp.stack(
        [src_len - core * enc_count, src_len - (1 - core) * enc_count, tgt_len - core * rows]
    ).astype(jnp.int32)
    own_side = core.reshape(1).astype(jnp.int32)
    far_side = 1 - own_side

    states = lax.all_gather(dec_states, "head")
    far_keys = lax.ppermute(enc_keys, "ctx", PARTNERS)
    far_values = lax.ppermute(enc_values, "ctx", PARTNERS)

    pieces = jnp.broadcast_to(
        jnp.concatenate([w_query, w_out], axis=1)[None], (NZ, piece, 2 * width)
    )
    pieces = lax.all_to_all(pieces, "ctx", 0, 0, axis_index_groups=Z_GROUPS)
    wq = pieces[:, :, :width]
    wo = pieces[:, :, width:]
    wo_own = lax.all_gather(wo, "ctx", axis_index_groups=X_GROUPS)

    wq_own = lax.all_to_all(
        jnp.broadcast_to(wq[None], (NX, NZ, piece, width)), "ctx", 0, 0, axis_index_groups=X_GROUPS
    )
    normed = normalize(states, norm_gain.reshape(heads, 1, width))
    wq_own, normed, far_keys, far_values, counts, own_side, far_side = lax.optimization_barrier(
        (wq_own, normed, far_keys, far_values, counts, own_side, far_side)
    )
    wq_far = lax.ppermute(wq_own, "ctx", PARTNERS)
    wo_far = lax.ppermute(wo_own, "ctx", PARTNERS)

    queries = query_part(own_side, normed, wq_own)
    queries = query_part(far_side, normed, wq_far, queries)
    gathered, start = [], 0
    for pairs in CUTS:
        attended = attend(
            counts, queries, enc_keys, enc_values, far_keys, far_values, start, pairs
        )
        gathered.append(lax.all_gather(attended, "head"))
        start += pairs
    return output_product(own_side, gathered, wo_own, wo_far)


def solution(mesh):
    placed = (
        P("ctx", "head"),
        P(),
        P("ctx", "head"),
        P("ctx", "head"),
        P("ctx", "head"),
        P("ctx", "head"),
        P(),
        P(),
    )
    return jax.shard_map(
        local, mesh=mesh, in_specs=placed, out_specs=P("ctx", "head"), check_vma=False
    )
```

```python
import functools

import jax
import jax.numpy as jnp
from jax import lax
from jax.experimental import pallas as pl
from jax.experimental.pallas import tpu as pltpu
from jax.sharding import PartitionSpec as P

DK = 64
NX, NZ = 4, 8
CUTS = (3, 1)


def place(x, z, core):
    return ((x % NX) * NZ + z % NZ) * 2 + core


def along_x(shift):
    return [
        (place(x, z, core), place(x + shift, z, core))
        for x in range(NX)
        for z in range(NZ)
        for core in range(2)
    ]


PARTNERS = [(i, i ^ 1) for i in range(2 * NX * NZ)]
Z_GROUPS = [[place(x, z, core) for z in range(NZ)] for x in range(NX) for core in range(2)]
X_GROUPS = [[place(x, z, core) for x in range(NX)] for z in range(NZ) for core in range(2)]


def normalize_kernel(x_ref, gain_ref, o_ref):
    blocks, rows, width = x_ref.shape
    square = jnp.zeros((rows, width), jnp.float32)
    for b in range(blocks):
        part = x_ref[b].astype(jnp.float32)
        square = square + part * part
    mean = jnp.sum(square, axis=1, keepdims=True) / (blocks * width)
    scale = lax.rsqrt(mean + 1e-06)
    first = lax.broadcasted_iota(jnp.int32, (1, 2 * DK), 1) < DK
    for b in range(blocks):
        part = x_ref[b].astype(jnp.float32) * scale * gain_ref[b]
        for j in range(width // (4 * DK)):
            one = part[:, 4 * DK * j : 4 * DK * j + 2 * DK]
            two = part[:, 4 * DK * j + 2 * DK : 4 * DK * (j + 1)]
            lanes = slice(2 * DK * j, 2 * DK * (j + 1))
            even = jnp.where(first, one, pltpu.roll(two, DK, 1))
            odd = jnp.where(first, pltpu.roll(one, DK, 1), two)
            o_ref[0, b, :, lanes] = even.astype(jnp.bfloat16)
            o_ref[1, b, :, lanes] = odd.astype(jnp.bfloat16)


def normalize(x, gain):
    blocks, rows, width = x.shape
    tile = 64
    return pl.pallas_call(
        normalize_kernel,
        out_shape=jax.ShapeDtypeStruct((2, blocks, rows, width // 2), jnp.bfloat16),
        grid=(rows // tile,),
        in_specs=[
            pl.BlockSpec((blocks, tile, width), lambda i: (0, i, 0)),
            pl.BlockSpec((blocks, 1, width), lambda i: (0, 0, 0)),
        ],
        out_specs=pl.BlockSpec((2, blocks, tile, width // 2), lambda i: (0, 0, i, 0)),
        compiler_params=pltpu.CompilerParams(vmem_limit_bytes=58 << 20),
        cost_estimate=pl.CostEstimate(
            flops=8 * rows * blocks * width,
            bytes_accessed=4 * blocks * width * rows,
            transcendentals=rows,
        ),
        name="normalize",
    )(x, gain)


def query_kernel(side_ref, x_ref, w_ref, *refs):
    sum_ref = refs[0] if len(refs) == 5 else None
    o_ref, xs, w, sems = refs[-4:]
    blocks = xs.shape[0]
    each = blocks // NX
    x_copies, w_copies = [], []
    for i in range(NX):
        there = slice(i * each, (i + 1) * each)
        x_copies.append(
            pltpu.make_async_copy(x_ref.at[side_ref[0], there], xs.at[there], sems.at[0, i])
        )
        w_copies.append(pltpu.make_async_copy(w_ref.at[i], w.at[i], sems.at[1, i]))
    for i in range(NX):
        x_copies[i].start()
        w_copies[i].start()
    depth = NZ // each
    total = jnp.zeros(o_ref.shape, jnp.float32) if sum_ref is None else sum_ref[...]
    for i in range(NX):
        x_copies[i].wait()
        w_copies[i].wait()
        for j in range(each):
            part = w[i, j * depth : (j + 1) * depth].reshape(xs.shape[2], o_ref.shape[1])
            total = total + jnp.dot(xs[i * each + j], part, preferred_element_type=jnp.float32)
    o_ref[...] = total.astype(o_ref.dtype)


def query_part(side, x, weights, partial=None):
    _, blocks, rows, half = x.shape
    piece, out = weights.shape[2:]
    whole = pl.BlockSpec((rows, out), lambda i, s: (0, 0))
    anywhere = pl.BlockSpec(memory_space=pl.ANY)
    more = [] if partial is None else [partial]
    return pl.pallas_call(
        query_kernel,
        out_shape=jax.ShapeDtypeStruct(
            (rows, out), jnp.float32 if partial is None else jnp.bfloat16
        ),
        grid_spec=pltpu.PrefetchScalarGridSpec(
            num_scalar_prefetch=1,
            grid=(1,),
            in_specs=[anywhere, anywhere] + [whole] * len(more),
            out_specs=whole,
            scratch_shapes=[
                pltpu.VMEM((blocks, rows, half), jnp.bfloat16),
                pltpu.VMEM((NX, NZ, piece, out), jnp.bfloat16),
                pltpu.SemaphoreType.DMA((2, NX)),
            ],
        ),
        compiler_params=pltpu.CompilerParams(vmem_limit_bytes=24 << 20),
        cost_estimate=pl.CostEstimate(
            flops=2 * rows * blocks * half * out,
            bytes_accessed=2 * blocks * half * (rows + out),
            transcendentals=0,
        ),
        name="query_part",
    )(side, x, weights, *more)


def output_kernel(n_in, side_ref, *refs):
    x_refs, (own_ref, far_ref, o_ref, xs, w, sems) = refs[:n_in], refs[n_in:]
    blocks, _, width = xs.shape
    core = side_ref[0]
    each = blocks // NX
    depth = NZ // each
    copies = []
    for i in range(NX):
        blocks_of = pl.ds(side_ref[1 + i] * each, each)
        group, at = [], 0
        for k, x_ref in enumerate(x_refs):
            lanes = slice(at, at + x_ref.shape[2])
            group.append(
                pltpu.make_async_copy(x_ref.at[blocks_of], xs.at[blocks_of, :, lanes], sems.at[i, k])
            )
            at += x_ref.shape[2]
        group.append(pltpu.make_async_copy(own_ref.at[:, i], w.at[i, :, core], sems.at[i, n_in]))
        group.append(
            pltpu.make_async_copy(far_ref.at[:, i], w.at[i, :, 1 - core], sems.at[i, n_in + 1])
        )
        copies.append(group)
    for group in copies:
        for copy in group:
            copy.start()
    acc = jnp.zeros(o_ref.shape, jnp.float32)
    for i in range(NX):
        for copy in copies[i]:
            copy.wait()
        for j in range(each):
            part = w[i, j * depth : (j + 1) * depth].reshape(width, o_ref.shape[1])
            x = xs[side_ref[1 + i] * each + j]
            acc = acc + jnp.dot(x, part, preferred_element_type=jnp.float32)
    o_ref[...] = acc.astype(jnp.bfloat16)


def output_product(side, xs, own, far):
    blocks, rows = xs[0].shape[:2]
    width = sum(x.shape[2] for x in xs)
    piece, out = own.shape[2:]
    anywhere = pl.BlockSpec(memory_space=pl.ANY)
    return pl.pallas_call(
        functools.partial(output_kernel, len(xs)),
        out_shape=jax.ShapeDtypeStruct((rows, out), jnp.bfloat16),
        grid_spec=pltpu.PrefetchScalarGridSpec(
            num_scalar_prefetch=1,
            grid=(1,),
            in_specs=[anywhere] * (len(xs) + 2),
            out_specs=pl.BlockSpec((rows, out), lambda i, s: (0, 0)),
            scratch_shapes=[
                pltpu.VMEM((blocks, rows, width), jnp.bfloat16),
                pltpu.VMEM((NX, NZ, 2, piece, out), jnp.bfloat16),
                pltpu.SemaphoreType.DMA((NX, len(xs) + 2)),
            ],
        ),
        compiler_params=pltpu.CompilerParams(vmem_limit_bytes=56 << 20),
        cost_estimate=pl.CostEstimate(
            flops=2 * rows * blocks * width * out,
            bytes_accessed=2 * blocks * width * (rows + out),
            transcendentals=0,
        ),
        name="output_product",
    )(side, *xs, own, far)


def attend_kernel(step, start, s_ref, q_ref, ko_ref, vo_ref, kf_ref, vf_ref, o_ref, keys, vals, sems):
    half = ko_ref.shape[0]
    rows = q_ref.shape[0]
    pair, tile = 2 * DK, 256
    turn, turns = pl.program_id(0), pl.num_programs(0)
    slot = lax.rem(turn, 2)

    def copies(h, into):
        lanes = pl.ds(pl.multiple_of((start + h) * pair, pair), pair)
        return [
            pltpu.make_async_copy(ko_ref.at[:, lanes], keys.at[into, :half], sems.at[into, 0]),
            pltpu.make_async_copy(kf_ref.at[:, lanes], keys.at[into, half:], sems.at[into, 1]),
            pltpu.make_async_copy(vo_ref.at[:, lanes], vals.at[into, :half, :pair], sems.at[into, 2]),
            pltpu.make_async_copy(vf_ref.at[:, lanes], vals.at[into, half:, :pair], sems.at[into, 3]),
        ]

    @pl.when(turn == 0)
    def _():
        for copy in copies(turn, slot):
            copy.start()
        for base, count in ((0, s_ref[0]), (half, s_ref[1])):
            for c in range(0, half, tile):
                valid = lax.broadcasted_iota(jnp.int32, (tile, pair), 0) + c < count
                ones = jnp.where(valid, 1.0, 0.0).astype(jnp.bfloat16)
                for into in range(2):
                    vals[into, base + c : base + c + tile, pair:] = ones

    @pl.when(turn + 1 < turns)
    def _():
        for copy in copies(turn + 1, 1 - slot):
            copy.start()

    def arrive(k, base, count):
        for copy in (copies(turn, slot)[k], copies(turn, slot)[k + 2]):
            copy.wait()
        for c in range(0, half, tile):

            @pl.when(c + tile > count)
            def _():
                there = slice(base + c, base + c + tile)
                valid = lax.broadcasted_iota(jnp.int32, (tile, 1), 0) + c < count
                keys[slot, there] = jnp.where(valid, keys[slot, there], keys[slot, base : base + 1])
                v = vals[slot, there, :pair]
                vals[slot, there, :pair] = jnp.where(valid, v, jnp.zeros_like(v))

    first = lax.broadcasted_iota(jnp.int32, (1, pair), 1) < DK
    q = q_ref[...]
    zero = jnp.zeros_like(q)
    both = jnp.concatenate([jnp.where(first, q, zero), jnp.where(first, zero, q)], axis=0)
    top = acc = None
    for c in range(0, 2 * half, step):
        if c == 0:
            arrive(0, 0, s_ref[0])
        if c == half:
            arrive(1, half, s_ref[1])
        scores = lax.dot_general(both, keys[slot, c : c + step], (((1,), (1,)), ((), ())), preferred_element_type=jnp.float32)
        new_top = jnp.max(scores, axis=1, keepdims=True)
        if top is not None:
            new_top = jnp.maximum(top, new_top)
        weights = jnp.exp(scores - new_top).astype(jnp.bfloat16)
        part = jnp.dot(weights, vals[slot, c : c + step], preferred_element_type=jnp.float32)
        acc = part if top is None else acc * jnp.exp(top - new_top) + part
        top = new_top
    out = acc[:, :pair] / acc[:, pair:]
    live = lax.broadcasted_iota(jnp.int32, (rows, 1), 0) < s_ref[2]
    o_ref[...] = jnp.where(live, jnp.where(first, out[:rows], out[rows:]), 0.0).astype(jnp.bfloat16)


def attend(counts, q, own_k, own_v, far_k, far_v, start, pairs):
    rows = q.shape[0]
    width = pairs * 2 * DK
    half = own_k.shape[0]
    pair = 2 * DK
    hbm = pl.BlockSpec(memory_space=pl.ANY)
    qs = pl.BlockSpec((rows, pair), lambda h, s: (0, start + h))
    os = pl.BlockSpec((rows, pair), lambda h, s: (0, h))
    return pl.pallas_call(
        functools.partial(attend_kernel, 512, start),
        out_shape=jax.ShapeDtypeStruct((rows, width), jnp.bfloat16),
        grid_spec=pltpu.PrefetchScalarGridSpec(
            num_scalar_prefetch=1,
            grid=(pairs,),
            in_specs=[qs, hbm, hbm, hbm, hbm],
            out_specs=os,
            scratch_shapes=[
                pltpu.VMEM((2, 2 * half, pair), jnp.bfloat16),
                pltpu.VMEM((2, 2 * half, 2 * pair), jnp.bfloat16),
                pltpu.SemaphoreType.DMA((2, 4)),
            ],
        ),
        compiler_params=pltpu.CompilerParams(vmem_limit_bytes=58 << 20),
        cost_estimate=pl.CostEstimate(
            flops=16 * rows * width * half,
            bytes_accessed=8 * half * width,
            transcendentals=2 * rows * width // DK * half,
        ),
        name="attend",
    )(counts, q, own_k, own_v, far_k, far_v)


def local(dec_states, norm_gain, w_query, enc_keys, enc_values, w_out, tgt_lengths, src_lengths):
    heads = lax.axis_size("head")
    position = lax.axis_index("ctx")
    core = position % 2
    example = position // 2
    rows, width = dec_states.shape
    piece = w_query.shape[0]
    enc_count = enc_keys.shape[0]
    slot_ids = jnp.arange(tgt_lengths.shape[0], dtype=jnp.int32)
    tgt_len = jnp.sum(jnp.where(slot_ids == example, tgt_lengths, 0))
    src_len = jnp.sum(jnp.where(slot_ids == example, src_lengths, 0))
    counts = jnp.stack(
        [src_len - core * enc_count, src_len - (1 - core) * enc_count, tgt_len - core * rows]
    ).astype(jnp.int32)
    own_side = core.reshape(1).astype(jnp.int32)
    far_side = 1 - own_side
    x = position // (2 * NZ)
    order = jnp.stack([core, x, (x - 1) % NX, (x + 1) % NX, (x + 2) % NX]).astype(jnp.int32)

    states = lax.all_gather(dec_states, "head")
    far_keys = lax.ppermute(enc_keys, "ctx", PARTNERS)
    far_values = lax.ppermute(enc_values, "ctx", PARTNERS)

    wq = lax.all_to_all(
        jnp.broadcast_to(w_query[None], (NZ, piece, width)), "ctx", 0, 0, axis_index_groups=Z_GROUPS
    )
    wo = jnp.stack([w_out] + [lax.ppermute(w_out, "ctx", along_x(shift)) for shift in (1, -1, 2)])
    wq, wo = lax.optimization_barrier((wq, wo))
    wo_own = lax.all_gather(wo, "ctx", axis_index_groups=Z_GROUPS)

    wq_own = lax.all_to_all(
        jnp.broadcast_to(wq[None], (NX, NZ, piece, width)), "ctx", 0, 0, axis_index_groups=X_GROUPS
    )
    normed = normalize(states, norm_gain.reshape(heads, 1, width))
    wq_own, normed, far_keys, far_values, counts, own_side, far_side, order = lax.optimization_barrier(
        (wq_own, normed, far_keys, far_values, counts, own_side, far_side, order)
    )
    wq_far = lax.ppermute(wq_own, "ctx", PARTNERS)
    wo_far = lax.ppermute(wo_own, "ctx", PARTNERS)

    queries = query_part(own_side, normed, wq_own)
    queries = query_part(far_side, normed, wq_far, queries)
    gathered, start = [], 0
    for pairs in CUTS:
        attended = attend(
            counts, queries, enc_keys, enc_values, far_keys, far_values, start, pairs
        )
        gathered.append(lax.all_gather(attended, "head"))
        start += pairs
    return output_product(order, gathered, wo_own, wo_far)


def solution(mesh):
    placed = (
        P("ctx", "head"),
        P(),
        P("ctx", "head"),
        P("ctx", "head"),
        P("ctx", "head"),
        P("ctx", "head"),
        P(),
        P(),
    )
    return jax.shard_map(
        local, mesh=mesh, in_specs=placed, out_specs=P("ctx", "head"), check_vma=False
    )
```

```python
import functools

import jax
import jax.numpy as jnp
from jax import lax
from jax.experimental import pallas as pl
from jax.experimental.pallas import tpu as pltpu
from jax.sharding import PartitionSpec as P

DK = 64
NX, NZ = 4, 8
CUTS = (144, 112)


def place(x, z, core):
    return ((x % NX) * NZ + z % NZ) * 2 + core


def along_x(shift):
    return [
        (place(x, z, core), place(x + shift, z, core))
        for x in range(NX)
        for z in range(NZ)
        for core in range(2)
    ]


PARTNERS = [(i, i ^ 1) for i in range(2 * NX * NZ)]
Z_GROUPS = [[place(x, z, core) for z in range(NZ)] for x in range(NX) for core in range(2)]
X_GROUPS = [[place(x, z, core) for x in range(NX)] for z in range(NZ) for core in range(2)]


def normalize_kernel(x_ref, gain_ref, o_ref):
    blocks, rows, width = x_ref.shape
    square = jnp.zeros((rows, width), jnp.float32)
    for b in range(blocks):
        part = x_ref[b].astype(jnp.float32)
        square = square + part * part
    mean = jnp.sum(square, axis=1, keepdims=True) / (blocks * width)
    scale = lax.rsqrt(mean + 1e-06)
    first = lax.broadcasted_iota(jnp.int32, (1, 2 * DK), 1) < DK
    for b in range(blocks):
        part = x_ref[b].astype(jnp.float32) * scale * gain_ref[b]
        for j in range(width // (4 * DK)):
            one = part[:, 4 * DK * j : 4 * DK * j + 2 * DK]
            two = part[:, 4 * DK * j + 2 * DK : 4 * DK * (j + 1)]
            lanes = slice(2 * DK * j, 2 * DK * (j + 1))
            even = jnp.where(first, one, pltpu.roll(two, DK, 1))
            odd = jnp.where(first, pltpu.roll(one, DK, 1), two)
            o_ref[0, b, :, lanes] = even.astype(jnp.bfloat16)
            o_ref[1, b, :, lanes] = odd.astype(jnp.bfloat16)


def normalize(x, gain):
    blocks, rows, width = x.shape
    tile = 64
    return pl.pallas_call(
        normalize_kernel,
        out_shape=jax.ShapeDtypeStruct((2, blocks, rows, width // 2), jnp.bfloat16),
        grid=(rows // tile,),
        in_specs=[
            pl.BlockSpec((blocks, tile, width), lambda i: (0, i, 0)),
            pl.BlockSpec((blocks, 1, width), lambda i: (0, 0, 0)),
        ],
        out_specs=pl.BlockSpec((2, blocks, tile, width // 2), lambda i: (0, 0, i, 0)),
        compiler_params=pltpu.CompilerParams(vmem_limit_bytes=58 << 20),
        cost_estimate=pl.CostEstimate(
            flops=8 * rows * blocks * width,
            bytes_accessed=4 * blocks * width * rows,
            transcendentals=rows,
        ),
        name="normalize",
    )(x, gain)


def query_kernel(side_ref, x_ref, w_ref, *refs):
    sum_ref = refs[0] if len(refs) == 5 else None
    o_ref, xs, w, sems = refs[-4:]
    blocks = xs.shape[0]
    each = blocks // NX
    x_copies, w_copies = [], []
    for i in range(NX):
        there = slice(i * each, (i + 1) * each)
        x_copies.append(
            pltpu.make_async_copy(x_ref.at[side_ref[0], there], xs.at[there], sems.at[0, i])
        )
        w_copies.append(pltpu.make_async_copy(w_ref.at[i], w.at[i], sems.at[1, i]))
    for i in range(NX):
        x_copies[i].start()
        w_copies[i].start()
    depth = NZ // each
    total = jnp.zeros(o_ref.shape, jnp.float32) if sum_ref is None else sum_ref[...]
    for i in range(NX):
        x_copies[i].wait()
        w_copies[i].wait()
        for j in range(each):
            part = w[i, j * depth : (j + 1) * depth].reshape(xs.shape[2], o_ref.shape[1])
            total = total + jnp.dot(xs[i * each + j], part, preferred_element_type=jnp.float32)
    o_ref[...] = total.astype(o_ref.dtype)


def query_part(side, x, weights, partial=None):
    _, blocks, rows, half = x.shape
    piece, out = weights.shape[2:]
    whole = pl.BlockSpec((rows, out), lambda i, s: (0, 0))
    anywhere = pl.BlockSpec(memory_space=pl.ANY)
    more = [] if partial is None else [partial]
    return pl.pallas_call(
        query_kernel,
        out_shape=jax.ShapeDtypeStruct(
            (rows, out), jnp.float32 if partial is None else jnp.bfloat16
        ),
        grid_spec=pltpu.PrefetchScalarGridSpec(
            num_scalar_prefetch=1,
            grid=(1,),
            in_specs=[anywhere, anywhere] + [whole] * len(more),
            out_specs=whole,
            scratch_shapes=[
                pltpu.VMEM((blocks, rows, half), jnp.bfloat16),
                pltpu.VMEM((NX, NZ, piece, out), jnp.bfloat16),
                pltpu.SemaphoreType.DMA((2, NX)),
            ],
        ),
        compiler_params=pltpu.CompilerParams(vmem_limit_bytes=24 << 20),
        cost_estimate=pl.CostEstimate(
            flops=2 * rows * blocks * half * out,
            bytes_accessed=2 * blocks * half * (rows + out),
            transcendentals=0,
        ),
        name="query_part",
    )(side, x, weights, *more)


def output_kernel(n_in, side_ref, *refs):
    x_refs, (own_ref, far_ref, o_ref, xs, w, sems) = refs[:n_in], refs[n_in:]
    blocks, _, width = xs.shape
    core = side_ref[0]
    each = blocks // NX
    depth = NZ // each
    copies = []
    for i in range(NX):
        blocks_of = pl.ds(side_ref[1 + i] * each, each)
        group, at = [], 0
        for k, x_ref in enumerate(x_refs):
            part = slice(at, at + x_ref.shape[1])
            group.append(
                pltpu.make_async_copy(x_ref.at[blocks_of], xs.at[blocks_of, part], sems.at[i, k])
            )
            at += x_ref.shape[1]
        group.append(pltpu.make_async_copy(own_ref.at[:, i], w.at[i, :, core], sems.at[i, n_in]))
        group.append(
            pltpu.make_async_copy(far_ref.at[:, i], w.at[i, :, 1 - core], sems.at[i, n_in + 1])
        )
        copies.append(group)
    for group in copies:
        for copy in group:
            copy.start()
    acc = jnp.zeros(o_ref.shape, jnp.float32)
    for i in range(NX):
        for copy in copies[i]:
            copy.wait()
        for j in range(each):
            part = w[i, j * depth : (j + 1) * depth].reshape(width, o_ref.shape[1])
            x = xs[side_ref[1 + i] * each + j]
            acc = acc + jnp.dot(x, part, preferred_element_type=jnp.float32)
    o_ref[...] = acc.astype(jnp.bfloat16)


def output_product(side, xs, own, far):
    blocks, _, width = xs[0].shape
    rows = sum(x.shape[1] for x in xs)
    piece, out = own.shape[2:]
    anywhere = pl.BlockSpec(memory_space=pl.ANY)
    return pl.pallas_call(
        functools.partial(output_kernel, len(xs)),
        out_shape=jax.ShapeDtypeStruct((rows, out), jnp.bfloat16),
        grid_spec=pltpu.PrefetchScalarGridSpec(
            num_scalar_prefetch=1,
            grid=(1,),
            in_specs=[anywhere] * (len(xs) + 2),
            out_specs=pl.BlockSpec((rows, out), lambda i, s: (0, 0)),
            scratch_shapes=[
                pltpu.VMEM((blocks, rows, width), jnp.bfloat16),
                pltpu.VMEM((NX, NZ, 2, piece, out), jnp.bfloat16),
                pltpu.SemaphoreType.DMA((NX, len(xs) + 2)),
            ],
        ),
        compiler_params=pltpu.CompilerParams(vmem_limit_bytes=56 << 20),
        cost_estimate=pl.CostEstimate(
            flops=2 * rows * blocks * width * out,
            bytes_accessed=2 * blocks * width * (rows + out),
            transcendentals=0,
        ),
        name="output_product",
    )(side, *xs, own, far)


def attend_kernel(step, s_ref, q_ref, ko_ref, vo_ref, kf_ref, vf_ref, *refs):
    *o_refs, keys, vals, sems = refs
    half = ko_ref.shape[0]
    rows = q_ref.shape[0]
    pair, tile = 2 * DK, 256
    turn, turns = pl.program_id(0), pl.num_programs(0)
    slot = lax.rem(turn, 2)

    def copies(h, into):
        lanes = pl.ds(pl.multiple_of(h * pair, pair), pair)
        return [
            pltpu.make_async_copy(ko_ref.at[:, lanes], keys.at[into, :half], sems.at[into, 0]),
            pltpu.make_async_copy(kf_ref.at[:, lanes], keys.at[into, half:], sems.at[into, 1]),
            pltpu.make_async_copy(vo_ref.at[:, lanes], vals.at[into, :half, :pair], sems.at[into, 2]),
            pltpu.make_async_copy(vf_ref.at[:, lanes], vals.at[into, half:, :pair], sems.at[into, 3]),
        ]

    @pl.when(turn == 0)
    def _():
        for copy in copies(turn, slot):
            copy.start()
        for base, count in ((0, s_ref[0]), (half, s_ref[1])):
            for c in range(0, half, tile):
                valid = lax.broadcasted_iota(jnp.int32, (tile, pair), 0) + c < count
                ones = jnp.where(valid, 1.0, 0.0).astype(jnp.bfloat16)
                for into in range(2):
                    vals[into, base + c : base + c + tile, pair:] = ones

    @pl.when(turn + 1 < turns)
    def _():
        for copy in copies(turn + 1, 1 - slot):
            copy.start()

    def arrive(k, base, count):
        for copy in (copies(turn, slot)[k], copies(turn, slot)[k + 2]):
            copy.wait()
        for c in range(0, half, tile):

            @pl.when(c + tile > count)
            def _():
                there = slice(base + c, base + c + tile)
                valid = lax.broadcasted_iota(jnp.int32, (tile, 1), 0) + c < count
                keys[slot, there] = jnp.where(valid, keys[slot, there], keys[slot, base : base + 1])
                v = vals[slot, there, :pair]
                vals[slot, there, :pair] = jnp.where(valid, v, jnp.zeros_like(v))

    first = lax.broadcasted_iota(jnp.int32, (1, pair), 1) < DK
    q = q_ref[...]
    zero = jnp.zeros_like(q)
    both = jnp.concatenate([jnp.where(first, q, zero), jnp.where(first, zero, q)], axis=0)
    top = acc = None
    for c in range(0, 2 * half, step):
        if c == 0:
            arrive(0, 0, s_ref[0])
        if c == half:
            arrive(1, half, s_ref[1])
        scores = lax.dot_general(both, keys[slot, c : c + step], (((1,), (1,)), ((), ())), preferred_element_type=jnp.float32)
        new_top = jnp.max(scores, axis=1, keepdims=True)
        if top is not None:
            new_top = jnp.maximum(top, new_top)
        weights = jnp.exp(scores - new_top).astype(jnp.bfloat16)
        part = jnp.dot(weights, vals[slot, c : c + step], preferred_element_type=jnp.float32)
        acc = part if top is None else acc * jnp.exp(top - new_top) + part
        top = new_top
    out = acc[:, :pair] / acc[:, pair:]
    live = lax.broadcasted_iota(jnp.int32, (rows, 1), 0) < s_ref[2]
    out = jnp.where(live, jnp.where(first, out[:rows], out[rows:]), 0.0).astype(jnp.bfloat16)
    at = 0
    for o_ref in o_refs:
        o_ref[...] = out[at : at + o_ref.shape[0]]
        at += o_ref.shape[0]


def attend(counts, q, own_k, own_v, far_k, far_v, cuts):
    rows, width = q.shape
    half = own_k.shape[0]
    pair = 2 * DK
    hbm = pl.BlockSpec(memory_space=pl.ANY)
    qs = pl.BlockSpec((rows, pair), lambda h, s: (0, h))
    os = [pl.BlockSpec((cut, pair), lambda h, s: (0, h)) for cut in cuts]
    return pl.pallas_call(
        functools.partial(attend_kernel, 512),
        out_shape=[jax.ShapeDtypeStruct((cut, width), jnp.bfloat16) for cut in cuts],
        grid_spec=pltpu.PrefetchScalarGridSpec(
            num_scalar_prefetch=1,
            grid=(width // pair,),
            in_specs=[qs, hbm, hbm, hbm, hbm],
            out_specs=os,
            scratch_shapes=[
                pltpu.VMEM((2, 2 * half, pair), jnp.bfloat16),
                pltpu.VMEM((2, 2 * half, 2 * pair), jnp.bfloat16),
                pltpu.SemaphoreType.DMA((2, 4)),
            ],
        ),
        compiler_params=pltpu.CompilerParams(vmem_limit_bytes=58 << 20),
        cost_estimate=pl.CostEstimate(
            flops=16 * rows * width * half,
            bytes_accessed=8 * half * width,
            transcendentals=2 * rows * width // DK * half,
        ),
        name="attend",
    )(counts, q, own_k, own_v, far_k, far_v)


def local(dec_states, norm_gain, w_query, enc_keys, enc_values, w_out, tgt_lengths, src_lengths):
    heads = lax.axis_size("head")
    position = lax.axis_index("ctx")
    core = position % 2
    example = position // 2
    rows, width = dec_states.shape
    piece = w_query.shape[0]
    enc_count = enc_keys.shape[0]
    slot_ids = jnp.arange(tgt_lengths.shape[0], dtype=jnp.int32)
    tgt_len = jnp.sum(jnp.where(slot_ids == example, tgt_lengths, 0))
    src_len = jnp.sum(jnp.where(slot_ids == example, src_lengths, 0))
    counts = jnp.stack(
        [src_len - core * enc_count, src_len - (1 - core) * enc_count, tgt_len - core * rows]
    ).astype(jnp.int32)
    own_side = core.reshape(1).astype(jnp.int32)
    far_side = 1 - own_side
    x = position // (2 * NZ)
    order = jnp.stack([core, x, (x - 1) % NX, (x + 1) % NX, (x + 2) % NX]).astype(jnp.int32)

    states = lax.all_gather(dec_states, "head")
    far_keys = lax.ppermute(enc_keys, "ctx", PARTNERS)
    far_values = lax.ppermute(enc_values, "ctx", PARTNERS)

    wq = lax.all_to_all(
        jnp.broadcast_to(w_query[None], (NZ, piece, width)), "ctx", 0, 0, axis_index_groups=Z_GROUPS
    )
    wo = jnp.stack([w_out] + [lax.ppermute(w_out, "ctx", along_x(shift)) for shift in (1, -1, 2)])
    wq, wo = lax.optimization_barrier((wq, wo))
    wo_own = lax.all_gather(wo, "ctx", axis_index_groups=Z_GROUPS)

    wq_own = lax.all_to_all(
        jnp.broadcast_to(wq[None], (NX, NZ, piece, width)), "ctx", 0, 0, axis_index_groups=X_GROUPS
    )
    normed = normalize(states, norm_gain.reshape(heads, 1, width))
    wq_own, normed, far_keys, far_values, counts, own_side, far_side, order = lax.optimization_barrier(
        (wq_own, normed, far_keys, far_values, counts, own_side, far_side, order)
    )
    wq_far = lax.ppermute(wq_own, "ctx", PARTNERS)

    queries = query_part(own_side, normed, wq_own)
    queries = query_part(far_side, normed, wq_far, queries)
    attended = attend(counts, queries, enc_keys, enc_values, far_keys, far_values, CUTS)
    gathered = [lax.all_gather(part, "head") for part in attended]
    wo_own, _ = lax.optimization_barrier((wo_own, attended[1]))
    wo_far = lax.ppermute(wo_own, "ctx", PARTNERS)
    return output_product(order, gathered, wo_own, wo_far)


def solution(mesh):
    placed = (
        P("ctx", "head"),
        P(),
        P("ctx", "head"),
        P("ctx", "head"),
        P("ctx", "head"),
        P("ctx", "head"),
        P(),
        P(),
    )
    return jax.shard_map(
        local, mesh=mesh, in_specs=placed, out_specs=P("ctx", "head"), check_vma=False
    )
```
